32 devices in a mesh: dp: 8 (over y, x, core), seq: 4 (over z).
Axes of the slice: x: 2, y: 2, z: 4, core: 2. Of those that a mesh axis runs over, the one named last changes fastest.
Arguments:
- hidden_states: bfloat16 [8192, 1024], P(('dp', 'seq')), may hold values from -96 to 96
- cotangent: bfloat16 [8192, 1024], P(('dp', 'seq')), may hold values from -6 to 6
- w_qkv: bfloat16 [1024, 3072], P(('dp', 'seq')), may hold values from -0.1875 to 0.1875
- b_query: bfloat16 [1024], P(('dp', 'seq')), may hold values from -3 to 3
- b_value: bfloat16 [1024], P(('dp', 'seq')), may hold values from -0.29882812 to 0.29882812
- w_out: bfloat16 [1024, 1024], P(('dp', 'seq')), may hold values from -3 to 3
- b_out: bfloat16 [1024], P(('dp', 'seq')), may hold values from -3 to 3
- ln1_gain: bfloat16 [1024], P(('dp', 'seq')), may hold values from 0.099609375 to 1.8984375
- ln1_shift: bfloat16 [1024], P(('dp', 'seq')), may hold values from -2 to 2
- w_up: bfloat16 [1024, 4096], P(('dp', 'seq')), may hold values from -0.1875 to 0.1875
- b_up: bfloat16 [4096], P(('dp', 'seq')), may hold values from -3 to 3
- w_down: bfloat16 [1024, 4096], P(('dp', 'seq')), may hold values from -0.09375 to 0.09375
- b_down: bfloat16 [1024], P(('dp', 'seq')), may hold values from -3 to 3
- ln2_gain: bfloat16 [1024], P(('dp', 'seq')), may hold values from 0.099609375 to 1.8984375
- ln2_shift: bfloat16 [1024], P(('dp', 'seq')), may hold values from -2 to 2
Outputs:
- layer_out: bfloat16 [8192, 1024], P(('dp', 'seq'))
- grad_input: float32 [8192, 1024], P(('dp', 'seq'))
- grad_w_qkv: float32 [1024, 3072], P(('dp', 'seq'))
- grad_b_query: float32 [1024], P(('dp', 'seq'))
- grad_b_value: float32 [1024], P(('dp', 'seq'))
- grad_w_out: float32 [1024, 1024], P(('dp', 'seq'))
- grad_b_out: float32 [1024], P(('dp', 'seq'))
- grad_ln1_gain: float32 [1024], P(('dp', 'seq'))
- grad_ln1_shift: float32 [1024], P(('dp', 'seq'))
- grad_w_up: float32 [1024, 4096], P(('dp', 'seq'))
- grad_b_up: float32 [4096], P(('dp', 'seq'))
- grad_w_down: float32 [1024, 4096], P(('dp', 'seq'))
- grad_b_down: float32 [1024], P(('dp', 'seq'))
- grad_ln2_gain: float32 [1024], P(('dp', 'seq'))
- grad_ln2_shift: float32 [1024], P(('dp', 'seq'))
The draws below stay inside these ranges and needn't reach their ends.
All inputs are finite; a program needn't handle non-finite values.
Results may differ from the reference program's by a relative error of at most 0.018.
The reference program's roundings to bfloat16 on the way count: a program that leaves them out, or rounds other values in their place, can miss the bound.
Values may be sent and summed in bfloat16 or wider, within the bound.
No kernel may reach another device: no remote copies, remote signals or barrier semaphores. Data moves between devices by JAX's collectives and lax.ppermute only.
A program may use at most 192 MiB of HBM per device.

```python
import math
import jax
import jax.numpy as jnp
from jax import lax

D = 1024
H = 16
HD = 64
FF = 4096
SEQ_LEN = 1024
SEQS = 8
TOKENS = 8192
N_DP = 8
N_SEQ = 4


def draw_hidden_states(key, part):
    base_key, pair_key = jax.random.split(key, 2)
    owners = N_DP * N_SEQ
    values = jax.random.truncated_normal(base_key, -4.0, 4.0, (TOKENS, D), jnp.float32)
    pairing = jax.random.permutation(pair_key, owners)
    row_owner = jnp.arange(TOKENS) // (TOKENS // owners)
    col_owner = jnp.arange(D) // (D // owners)
    paired = pairing[row_owner][:, None] == col_owner[None, :]
    values = jnp.where(paired, 3.0 * values, values)
    return values.astype(jnp.bfloat16)


def strengthened(entries, rng, source, target, blocks, factor):
    owner, partner = [(jnp.arange(entries.shape[position]) // (entries.shape[position] // blocks)).reshape([-1 if axis == position else 1 for axis in range(entries.ndim)]) for position in (source, target)]
    chosen = jax.random.permutation(rng, blocks)[partner]
    strong = (owner == chosen) | (owner == (partner + blocks // 2) % blocks)
    return jnp.where(strong, factor * entries, entries)


def block_levels(key, extent, cuts, low, high):
    def one(position, blocks):
        steps = jax.random.uniform(jax.random.fold_in(jax.random.fold_in(key, 6), position), (blocks,), jnp.float32, low / len(cuts), high / len(cuts))
        return jnp.repeat(jnp.exp(steps), extent[position] // blocks).reshape((-1,) + (1,) * (len(extent) - position - 1))

    level = one(*cuts[0])
    for cut in cuts[1:]:
        level = level * one(*cut)
    return level


def gaussian(key, extent, deviation, most, cuts=(), kind=jnp.bfloat16):
    values = deviation * jax.random.normal(key, extent, jnp.float32)
    if cuts:
        values = values * block_levels(key, extent, cuts, -0.22, 0.18)
    return jnp.clip(values, -most, most).astype(kind)


def gaussian_with(own_key, extent, scale, most, cuts, heavy, kind=jnp.bfloat16):
    values = scale * jax.random.normal(own_key, extent, jnp.float32)
    if cuts:
        values = values * block_levels(own_key, extent, cuts, -0.22, 0.18)
    return jnp.clip(strengthened(values, jax.random.fold_in(own_key, 3), *heavy), -most, most).astype(kind)


def setup_inputs(seed: int = 0) -> dict:
    keys = jax.random.split(jax.random.key(seed), 16)
    return {
        "hidden_states": draw_hidden_states(jax.random.fold_in(keys[15], 71), 0),
        "cotangent": gaussian_with(keys[1], (TOKENS, D), 1.0, 6.0, ((0, 32),), (0, 1, 32, 2.75)),
        "w_qkv": gaussian(keys[2], (D, 3 * D), D ** -0.5, 0.1875, ((0, 32),)),
        "b_query": gaussian(keys[3], (D,), 0.5, 3.0, ((0, 32),)),
        "b_value": gaussian(keys[4], (D,), 0.05, 0.29882812, ((0, 32),)),
        "w_out": gaussian(keys[5], (D, D), (max(1, 4 * D // SEQ_LEN)) ** -0.5, 3.0, ((0, 32),)),
        "b_out": gaussian(keys[6], (D,), 0.5, 3.0, ((0, 32),)),
        "ln1_gain": jnp.clip(1.0 + 0.18 * jax.random.normal(keys[7], (D,), jnp.float32), 0.099609375, 1.8984375).astype(jnp.bfloat16),
        "ln1_shift": gaussian(keys[8], (D,), 0.3, 2.0, ((0, 32),)),
        "w_up": gaussian(keys[9], (D, FF), D ** -0.5, 0.1875, ((0, 32),)),
        "b_up": gaussian(keys[10], (FF,), 0.5, 3.0, ((0, 32),)),
        "w_down": gaussian(keys[11], (D, FF), FF ** -0.5, 0.09375, ((0, 32),)),
        "b_down": gaussian(keys[12], (D,), 0.5, 3.0, ((0, 32),)),
        "ln2_gain": jnp.clip(1.0 + 0.18 * jax.random.normal(keys[13], (D,), jnp.float32), 0.099609375, 1.8984375).astype(jnp.bfloat16),
        "ln2_shift": gaussian(keys[14], (D,), 0.3, 2.0, ((0, 32),)),
    }


EPS = 1e-12

def layer_norm(residual, gain_vec, shift_vec):
    row_mean = lax.optimization_barrier(jnp.mean(residual, -1, keepdims=True))
    centred = residual - row_mean
    variance = lax.optimization_barrier(jnp.mean(centred * centred, -1, keepdims=True))
    inv_std = lax.rsqrt(variance + EPS)
    normed = centred * inv_std
    return (normed * gain_vec + shift_vec, normed, inv_std)

def norm_back(incoming, normed, inv_std, gain_vec):
    scaled = incoming * gain_vec
    return inv_std * (scaled - lax.optimization_barrier(jnp.mean(scaled, -1, keepdims=True)) - normed * lax.optimization_barrier(jnp.mean(scaled * normed, -1, keepdims=True)))

def gelu_both(inner):
    normal_cdf = 0.5 * (1.0 + jax.scipy.special.erf(inner / math.sqrt(2.0)))
    gelu_value = inner * normal_cdf
    gelu_slope = normal_cdf + inner * jnp.exp(-0.5 * inner * inner) / math.sqrt(2.0 * math.pi)
    return (gelu_value, gelu_slope)

def contract_last(left, right):
    return lax.dot_general(left, right, (((1,), (1,)), ((), ())), preferred_element_type=jnp.float32)

def contract_first(left, right):
    return lax.dot_general(left, right, (((0,), (0,)), ((), ())), preferred_element_type=jnp.float32)

def attend_forward(query_heads, key_heads, value_heads, row_block):
    length, groups_here, head_dim = query_heads.shape
    score_scale = 1.0 / math.sqrt(head_dim)
    blocked = query_heads.reshape(length // row_block, row_block, groups_here, head_dim)
    key_wide = key_heads.astype(jnp.float32)
    value_wide = value_heads.astype(jnp.float32)

    def one_block(query_block):
        scores = jnp.einsum('qge,kge->gqk', query_block.astype(jnp.float32), key_wide) * score_scale
        row_max = lax.optimization_barrier(jnp.max(scores, -1, keepdims=True))
        log_total = row_max + jnp.log(lax.optimization_barrier(jnp.sum(jnp.exp(scores - row_max), -1, keepdims=True)))
        weights = jnp.exp(scores - log_total).astype(jnp.bfloat16)
        outputs = jnp.einsum('gqk,kge->qge', weights.astype(jnp.float32), value_wide)
        return (outputs.astype(jnp.bfloat16), log_total[:, :, 0])
    outputs, log_total = lax.map(one_block, blocked)
    return (outputs.reshape(length, groups_here, head_dim), log_total)

def attend_backward(query_heads, key_heads, value_heads, outputs, log_total, grad_out, row_block):
    length, groups_here, head_dim = query_heads.shape
    score_scale = 1.0 / math.sqrt(head_dim)
    count_blocks = length // row_block
    row_delta = lax.optimization_barrier(jnp.sum(grad_out.astype(jnp.float32) * outputs.astype(jnp.float32), -1))
    key_wide = key_heads.astype(jnp.float32)
    value_wide = value_heads.astype(jnp.float32)

    def blocks_of(tensor):
        return tensor.reshape((count_blocks, row_block) + tensor.shape[1:])

    def one_step(carried, pieces):
        grad_keys, grad_values = carried
        query_block, grad_block, total_block, delta_block = pieces
        query_wide = query_block.astype(jnp.float32)
        grad_wide = grad_block.astype(jnp.float32)
        scores = jnp.einsum('qge,kge->gqk', query_wide, key_wide) * score_scale
        probs = jnp.exp(scores - total_block[:, :, None])
        probs_low = probs.astype(jnp.bfloat16).astype(jnp.float32)
        grad_values = grad_values + jnp.einsum('gqk,qge->kge', probs_low, grad_wide)
        grad_probs = jnp.einsum('qge,kge->gqk', grad_wide, value_wide)
        grad_scores = (probs * (grad_probs - jnp.transpose(delta_block)[:, :, None])).astype(jnp.bfloat16)
        scores_wide = grad_scores.astype(jnp.float32)
        grad_query = jnp.einsum('gqk,kge->qge', scores_wide, key_wide) * score_scale
        grad_keys = grad_keys + jnp.einsum('gqk,qge->kge', scores_wide, query_wide) * score_scale
        return ((grad_keys, grad_values), grad_query.astype(jnp.bfloat16))
    zeros_init = jnp.zeros((length, groups_here, head_dim), jnp.float32)
    (grad_keys, grad_values), grad_query = lax.scan(one_step, (zeros_init, zeros_init), (blocks_of(query_heads), blocks_of(grad_out), log_total, blocks_of(row_delta)))
    return (grad_query.reshape(length, groups_here, head_dim), grad_keys.astype(jnp.bfloat16), grad_values.astype(jnp.bfloat16))

def reference(hidden_states, cotangent, w_qkv, b_query, b_value, w_out, b_out, ln1_gain, ln1_shift, w_up, b_up, w_down, b_down, ln2_gain, ln2_shift):
    row_block = min(512, SEQ_LEN)
    bias_front = jnp.concatenate([b_query.astype(jnp.float32), jnp.zeros((D,), jnp.float32), b_value.astype(jnp.float32)])
    gain_one = ln1_gain.astype(jnp.float32)
    gain_two = ln2_gain.astype(jnp.float32)

    def heads_of(tensor):
        return tensor.reshape(SEQ_LEN, H, HD)

    def one_seq(totals, pieces):
        seq_in, seq_cot = pieces
        projected = (jnp.dot(seq_in, w_qkv, preferred_element_type=jnp.float32) + bias_front).astype(jnp.bfloat16)
        query_heads = heads_of(projected[:, :D])
        key_heads = heads_of(projected[:, D:2 * D])
        value_heads = heads_of(projected[:, 2 * D:])
        outputs, log_total = attend_forward(query_heads, key_heads, value_heads, row_block)
        attn_flat = outputs.reshape(SEQ_LEN, D)
        resid_one = seq_in.astype(jnp.float32) + jnp.dot(attn_flat, w_out, preferred_element_type=jnp.float32) + b_out.astype(jnp.float32)
        hidden_one, normed_one, inv_one = layer_norm(resid_one, gain_one, ln1_shift.astype(jnp.float32))
        hidden_low = hidden_one.astype(jnp.bfloat16)
        inner = jnp.dot(hidden_low, w_up, preferred_element_type=jnp.float32) + b_up.astype(jnp.float32)
        gelu_value, gelu_slope = gelu_both(inner)
        active_low = gelu_value.astype(jnp.bfloat16)
        resid_two = hidden_one + contract_last(active_low, w_down) + b_down.astype(jnp.float32)
        layer_val, normed_two, inv_two = layer_norm(resid_two, gain_two, ln2_shift.astype(jnp.float32))
        grad_y = seq_cot.astype(jnp.float32)
        grad_gain_two = lax.optimization_barrier(jnp.sum(grad_y * normed_two, 0))
        grad_shift_two = lax.optimization_barrier(jnp.sum(grad_y, 0))
        grad_resid_two = norm_back(grad_y, normed_two, inv_two, gain_two)
        grad_low_two = grad_resid_two.astype(jnp.bfloat16)
        grad_bias_down = lax.optimization_barrier(jnp.sum(grad_resid_two, 0))
        grad_down = contract_first(grad_low_two, active_low)
        grad_inner = jnp.dot(grad_low_two, w_down, preferred_element_type=jnp.float32) * gelu_slope
        grad_inner_low = grad_inner.astype(jnp.bfloat16)
        grad_bias_up = lax.optimization_barrier(jnp.sum(grad_inner, 0))
        grad_up = contract_first(hidden_low, grad_inner_low)
        grad_hidden = grad_resid_two + contract_last(grad_inner_low, w_up)
        grad_gain_one = lax.optimization_barrier(jnp.sum(grad_hidden * normed_one, 0))
        grad_shift_one = lax.optimization_barrier(jnp.sum(grad_hidden, 0))
        grad_resid_one = norm_back(grad_hidden, normed_one, inv_one, gain_one)
        grad_low_one = grad_resid_one.astype(jnp.bfloat16)
        grad_bias_out = lax.optimization_barrier(jnp.sum(grad_resid_one, 0))
        grad_out_w = contract_first(attn_flat, grad_low_one)
        grad_attn = contract_last(grad_low_one, w_out).astype(jnp.bfloat16)
        grad_query, grad_keys, grad_values = attend_backward(query_heads, key_heads, value_heads, outputs, log_total, heads_of(grad_attn), row_block)
        grad_projected = jnp.concatenate([grad_query.reshape(SEQ_LEN, D), grad_keys.reshape(SEQ_LEN, D), grad_values.reshape(SEQ_LEN, D)], 1)
        grad_bias_query = lax.optimization_barrier(jnp.sum(grad_projected[:, :D].astype(jnp.float32), 0))
        grad_bias_value = lax.optimization_barrier(jnp.sum(grad_projected[:, 2 * D:].astype(jnp.float32), 0))
        grad_qkv_w = contract_first(seq_in, grad_projected)
        grad_in = grad_resid_one + contract_last(grad_projected, w_qkv)
        added = (grad_qkv_w, grad_bias_query, grad_bias_value, grad_out_w, grad_bias_out, grad_gain_one, grad_shift_one, grad_up, grad_bias_up, grad_down, grad_bias_down, grad_gain_two, grad_shift_two)
        totals = tuple((total + extra for total, extra in zip(totals, added)))
        return (totals, (layer_val.astype(jnp.bfloat16), grad_in))
    zero_totals = (jnp.zeros((D, 3 * D), jnp.float32), jnp.zeros((D,), jnp.float32), jnp.zeros((D,), jnp.float32), jnp.zeros((D, D), jnp.float32), jnp.zeros((D,), jnp.float32), jnp.zeros((D,), jnp.float32), jnp.zeros((D,), jnp.float32), jnp.zeros((D, FF), jnp.float32), jnp.zeros((FF,), jnp.float32), jnp.zeros((D, FF), jnp.float32), jnp.zeros((D,), jnp.float32), jnp.zeros((D,), jnp.float32), jnp.zeros((D,), jnp.float32))
    totals, (layer_all, grad_all) = lax.scan(one_seq, zero_totals, (hidden_states.reshape(SEQS, SEQ_LEN, D), cotangent.reshape(SEQS, SEQ_LEN, D)))
    return (layer_all.reshape(TOKENS, D), grad_all.reshape(TOKENS, D), totals[0], totals[1], totals[2], totals[3], totals[4], totals[5], totals[6], totals[7], totals[8], totals[9], totals[10], totals[11], totals[12])
```

```python
import functools
import math

import jax
import jax.numpy as jnp
from jax import lax
from jax.experimental import pallas as pl
from jax.experimental.pallas import tpu as pltpu
from jax.sharding import Mesh
from jax.sharding import PartitionSpec as P

HD = 64
EPS = 1e-12
ALL = ("y", "x", "core", "seq")
BF16 = jnp.bfloat16
F32 = jnp.float32


def layer_norm(residual, gain_vec, shift_vec):
    row_mean = jnp.mean(residual, -1, keepdims=True)
    centred = residual - row_mean
    variance = jnp.mean(centred * centred, -1, keepdims=True)
    inv_std = lax.rsqrt(variance + EPS)
    normed = centred * inv_std
    return (normed * gain_vec + shift_vec, normed, inv_std)


def norm_back(incoming, normed, inv_std, gain_vec):
    scaled = incoming * gain_vec
    return inv_std * (
        scaled
        - jnp.mean(scaled, -1, keepdims=True)
        - normed * jnp.mean(scaled * normed, -1, keepdims=True)
    )


def gelu_both(inner):
    normal_cdf = 0.5 * (1.0 + jax.scipy.special.erf(inner / math.sqrt(2.0)))
    gelu_value = inner * normal_cdf
    gelu_slope = normal_cdf + inner * jnp.exp(-0.5 * inner * inner) / math.sqrt(2.0 * math.pi)
    return (gelu_value, gelu_slope)


def dot(left, right):
    return jnp.dot(left, right, preferred_element_type=F32)


def contract_last(left, right):
    return lax.dot_general(left, right, (((1,), (1,)), ((), ())), preferred_element_type=F32)


def contract_first(left, right):
    return lax.dot_general(left, right, (((0,), (0,)), ((), ())), preferred_element_type=F32)


def lanes_of(head, shape):
    lane = lax.broadcasted_iota(jnp.int32, shape, len(shape) - 1)
    return (lane >= head * HD) & (lane < (head + 1) * HD)


def forward_kernel(score_scale, query_ref, key_ref, value_ref, out_ref, total_ref, value_t, out_t):
    head = pl.program_id(1)

    @pl.when((pl.program_id(0) == 0) & (head == 0))
    def _():
        value_t[...] = value_ref[...].astype(F32).T.astype(BF16)

    query = query_ref[...]
    query = jnp.where(lanes_of(head, query.shape), query, jnp.zeros_like(query))
    scores = contract_last(key_ref[...], query) * score_scale
    top = jnp.max(scores, 0, keepdims=True)
    weights = jnp.exp(scores - top)
    total = jnp.sum(weights, 0, keepdims=True)
    total_ref[pl.ds(head, 1), :] = top + jnp.log(total)
    probs = (weights * (1.0 / total)).astype(BF16)
    rows = pl.ds(pl.multiple_of(head * HD, HD), HD)
    out_t[rows, :] = dot(value_t[rows, :], probs)

    @pl.when(head == pl.num_programs(1) - 1)
    def _():
        out_ref[...] = out_t[...].T.astype(BF16)


def attend_forward(projected):
    length, width = projected.shape[0], projected.shape[1] // 3
    block = min(256, length)
    heads = width // HD
    return pl.pallas_call(
        functools.partial(forward_kernel, 1.0 / math.sqrt(HD)),
        grid=(length // block, heads),
        in_specs=[
            pl.BlockSpec((block, width), lambda i, h: (i, 0)),
            pl.BlockSpec((length, width), lambda i, h: (0, 1)),
            pl.BlockSpec((length, width), lambda i, h: (0, 2)),
        ],
        out_specs=[
            pl.BlockSpec((block, width), lambda i, h: (i, 0)),
            pl.BlockSpec((heads, block), lambda i, h: (0, i)),
        ],
        out_shape=[
            jax.ShapeDtypeStruct((length, width), BF16),
            jax.ShapeDtypeStruct((heads, length), F32),
        ],
        scratch_shapes=[pltpu.VMEM((width, length), BF16), pltpu.VMEM((width, block), F32)],
        compiler_params=pltpu.CompilerParams(vmem_limit_bytes=24 * 2**20),
        cost_estimate=pl.CostEstimate(
            flops=4 * length * length * width,
            bytes_accessed=8 * length * width,
            transcendentals=heads * length * length,
        ),
        name="attend_forward",
    )(projected, projected, projected)


def backward_kernel(score_scale, block, query_ref, key_ref, value_ref, out_ref, total_ref,
                    grad_ref, result_ref, key_t, delta, query_t):
    step, head = pl.program_id(0), pl.program_id(1)
    width = query_ref.shape[1]
    heads = width // HD
    blocks = key_t.shape[0]

    @pl.when((step == 0) & (head == 0))
    def _():
        for number in range(blocks):
            key_t[number] = key_ref[pl.ds(number * block, block), :].astype(F32).T.astype(BF16)
        product = (grad_ref[...].astype(F32) * out_ref[...].astype(F32)).T
        for number in range(heads):
            delta[pl.ds(number, 1), :] = jnp.sum(
                product[number * HD : (number + 1) * HD], 0, keepdims=True
            )

    here = pl.ds(pl.multiple_of(step * block, block), block)
    mask = lanes_of(head, (block, width))
    key, value = key_ref[here, :], value_ref[here, :]
    key = jnp.where(mask, key, jnp.zeros_like(key))
    value = jnp.where(mask, value, jnp.zeros_like(value))
    scores = contract_last(key, query_ref[...]) * score_scale
    probs = jnp.exp(scores - total_ref[pl.ds(head, 1), :])
    grad_value = dot(probs.astype(BF16), grad_ref[...])
    grad_probs = contract_last(value, grad_ref[...])
    grad_scores = (probs * (grad_probs - delta[pl.ds(head, 1), :])).astype(BF16)
    grad_key = dot(grad_scores, query_ref[...]) * score_scale
    rows = pl.ds(pl.multiple_of(head * HD, HD), HD)
    part = dot(key_t[step, rows, :], grad_scores)

    @pl.when(step == 0)
    def _():
        query_t[rows, :] = part

    @pl.when(step > 0)
    def _():
        query_t[rows, :] += part

    for place, piece in ((width, grad_key), (2 * width, grad_value)):
        low = piece.astype(BF16)
        held = result_ref[here, place : place + width]
        result_ref[here, place : place + width] = jnp.where(mask, low, held)

    @pl.when((step == pl.num_programs(0) - 1) & (head == heads - 1))
    def _():
        result_ref[:, :width] = (query_t[...] * score_scale).T.astype(BF16)


def attend_backward(projected, outputs, log_total, grad_out):
    length, width = outputs.shape
    block = min(256, length)
    heads = width // HD
    full = pl.BlockSpec((length, width), lambda i, h: (0, 0))
    return pl.pallas_call(
        functools.partial(backward_kernel, 1.0 / math.sqrt(HD), block),
        grid=(length // block, heads),
        in_specs=[
            full,
            pl.BlockSpec((length, width), lambda i, h: (0, 1)),
            pl.BlockSpec((length, width), lambda i, h: (0, 2)),
            full,
            pl.BlockSpec((heads, length), lambda i, h: (0, 0)),
            full,
        ],
        out_specs=pl.BlockSpec((length, 3 * width), lambda i, h: (0, 0)),
        out_shape=jax.ShapeDtypeStruct((length, 3 * width), BF16),
        scratch_shapes=[
            pltpu.VMEM((length // block, width, block), BF16),
            pltpu.VMEM((heads, length), F32),
            pltpu.VMEM((width, length), F32),
        ],
        compiler_params=pltpu.CompilerParams(vmem_limit_bytes=32 * 2**20),
        cost_estimate=pl.CostEstimate(
            flops=10 * length * length * width,
            bytes_accessed=16 * length * width,
            transcendentals=heads * length * length,
        ),
        name="attend_backward",
    )(projected, projected, projected, outputs, log_total, grad_out)


def shift(block, axis, size, distance):
    return lax.ppermute(block, axis, [(i, (i + distance) % size) for i in range(size)])


def after(value, *earlier):
    return lax.optimization_barrier((value,) + earlier)[0]


def shifts(block, axis, size):
    return [shift(block, axis, size, size - d) for d in range(1, size)]


def in_order(block, others, axis, size, dim):
    if size == 1:
        return jnp.expand_dims(block, dim)
    me = lax.axis_index(axis)
    if size == 2:
        low = jnp.where(me == 0, block, others[0])
        high = jnp.where(me == 0, others[0], block)
        return jnp.stack([low, high], dim)
    ahead = [block] + list(others)
    twice = jnp.stack(ahead + ahead, dim)
    return lax.dynamic_slice_in_dim(twice, lax.rem(size - me, size), size, dim)


def gather_blocks(block, axis, size, dim):
    return in_order(block, shifts(block, axis, size), axis, size, dim)


def pick(blocks, index, dim):
    if blocks.shape[dim] == 2:
        first = lax.index_in_dim(blocks, 0, dim, keepdims=False)
        second = lax.index_in_dim(blocks, 1, dim, keepdims=False)
        return jnp.where(index == 0, first, second)
    return lax.dynamic_index_in_dim(blocks, index, dim, keepdims=False)


def reduce_blocks(blocks, axis, size, dim):
    me = lax.axis_index(axis)
    total = pick(blocks, me, dim).astype(F32)
    for distance in range(1, size):
        sent = pick(blocks, lax.rem(me + distance, size), dim).astype(BF16)
        total = total + shift(sent, axis, size, distance).astype(F32)
    return total


def body(sizes, hidden_states, cotangent, w_qkv, b_query, b_value, w_out, b_out, ln1_gain,
         ln1_shift, w_up, b_up, w_down, b_down, ln2_gain, ln2_shift):
    ny, nx, nc, ns = sizes
    devices = ny * nx * nc * ns
    rows, width = w_out.shape
    tokens = hidden_states.shape[0]
    inner_width = w_up.shape[1]
    own = width // ns
    seq_at = lax.axis_index("seq")
    core_at = lax.axis_index("core")

    def halves(matrix):
        half = matrix.shape[-1] // nc
        parts = matrix.reshape(matrix.shape[:-1] + (nc, half))
        return pick(parts, core_at, parts.ndim - 2), pick(parts, nc - 1 - core_at, parts.ndim - 2)

    def swap(block):
        return shift(block, "core", nc, 1)

    def pair(block):
        return jnp.concatenate([block, swap(block)], 0)

    def own_tokens(part):
        return part[:tokens] + swap(part[tokens:])

    def own_columns(shard):
        kept, sent = halves(shard)
        return in_order(kept, [swap(sent)], "core", nc, 0)

    def line_of(block, others):
        line = in_order(block, others, "seq", ns, 1)
        return line.reshape(block.shape[0], ns * block.shape[1], block.shape[2])

    def plane_of(line):
        low_x = shifts(line[0], "x", nx)
        high_y = shifts(line[1], "y", ny)
        low = in_order(line[0], low_x, "x", nx, 0)
        high = in_order(line[1], high_y, "y", ny, 0)
        low_y = shifts(low, "y", ny)
        high_x = shifts(high, "x", nx)
        low = in_order(low, low_y, "y", ny, 0)
        high = in_order(high, high_x, "x", nx, 1)
        return jnp.stack([low, high], 2).reshape(ny * nx * nc * line.shape[1], line.shape[2])

    def over_plane(full):
        line_rows = full.shape[0] // (ny * nx * nc)
        parts = full.reshape(ny, nx, nc, line_rows, full.shape[1])
        low = reduce_blocks(parts[:, :, 0], "x", nx, 1).astype(BF16)
        high = reduce_blocks(parts[:, :, 1], "y", ny, 0).astype(BF16)
        low = reduce_blocks(low, "y", ny, 0).astype(BF16)
        high = reduce_blocks(high, "x", nx, 0).astype(BF16)
        return jnp.stack([low, high], 0)

    def over_line(part):
        blocks = part.reshape(nc, ns, part.shape[1] // ns, part.shape[2])
        total = reduce_blocks(blocks, "seq", ns, 1)
        kept = pick(total, core_at, 0)
        came = swap(pick(total, nc - 1 - core_at, 0).astype(BF16)).astype(F32)
        low = jnp.where(core_at == 0, kept, came)
        high = jnp.where(core_at == 0, came, kept)
        return jnp.concatenate([low, high], 1)

    small = (b_query, b_value, b_out, ln1_gain, ln1_shift, b_up, b_down, ln2_gain, ln2_shift)
    packed = jnp.concatenate(small)[None]
    packed = lax.all_to_all(
        jnp.tile(packed, (devices, 1)), ALL, split_axis=0, concat_axis=0, tiled=True
    ).astype(F32)
    vectors, place = [], 0
    for shard in small:
        vectors.append(packed[:, place : place + shard.shape[0]].reshape(-1))
        place += shard.shape[0]
    (bias_query, bias_value, bias_out, gain_one, shift_one, bias_up, bias_down, gain_two,
     shift_two) = vectors

    by_owner = w_qkv.reshape(rows, 3, ns, own).transpose(0, 2, 1, 3).reshape(rows, 3 * width)
    to_owner = by_owner.reshape(rows, ns, 3 * own)
    kept = lax.dynamic_index_in_dim(to_owner, seq_at, 1, keepdims=False)
    came = [
        shift(
            lax.dynamic_index_in_dim(to_owner, lax.rem(seq_at + ns - d, ns), 1, keepdims=False),
            "seq", ns, ns - d,
        )
        for d in range(1, ns)
    ]
    own_line = in_order(kept, came, "seq", ns, 0).reshape(ns * rows, 3 * own)
    plane = gather_blocks(gather_blocks(own_line, "x", nx, 0), "y", ny, 0)
    own_qkv = gather_blocks(plane, "core", nc, 2).reshape(width, 3 * own)

    up_out = own_columns(w_up), own_columns(w_out)
    up_out = after(jnp.concatenate(up_out, 2), *came)
    up_line = shifts(up_out, "seq", ns)
    hidden_sent = after(hidden_states, *up_line)
    hidden_line = shifts(hidden_sent, "seq", ns)
    seq_hidden = in_order(hidden_sent, hidden_line, "seq", ns, 0).reshape(ns * tokens, width)
    down_own = after(own_columns(w_down), *hidden_line)
    down_line = shifts(down_own, "seq", ns)
    half_up_out = plane_of(after(line_of(up_out, up_line), own_qkv))
    half = inner_width // nc
    half_up, half_out = half_up_out[:, :half], half_up_out[:, half:]
    other_out = swap(half_out)
    half_down = plane_of(after(line_of(down_own, down_line), half_up_out))

    own_bias = jnp.concatenate(
        [
            lax.dynamic_slice_in_dim(bias_query, seq_at * own, own),
            jnp.zeros((own,), F32),
            lax.dynamic_slice_in_dim(bias_value, seq_at * own, own),
        ]
    )
    projected = (dot(seq_hidden, own_qkv) + own_bias).astype(BF16)
    outputs, log_total = attend_forward(projected)
    attn_tok = lax.all_to_all(outputs, "seq", split_axis=0, concat_axis=1, tiled=True)
    qkv_own = after(own_columns(by_owner), attn_tok)
    qkv_line = shifts(qkv_own, "seq", ns)
    half_qkv = plane_of(after(line_of(qkv_own, qkv_line), half_down))
    other_qkv = swap(half_qkv)

    mixed, mixed_other = dot(attn_tok, half_out), dot(attn_tok, other_out)
    mixed = jnp.concatenate(
        [
            jnp.where(core_at == 0, mixed, mixed_other),
            jnp.where(core_at == 0, mixed_other, mixed),
        ],
        1,
    )
    resid_one = hidden_states.astype(F32) + mixed + bias_out
    hidden_one, normed_one, inv_one = layer_norm(resid_one, gain_one, shift_one)
    hidden_low = hidden_one.astype(BF16)

    hidden_two = pair(hidden_low)
    gelu_value, gelu_slope = gelu_both(dot(hidden_two, half_up) + halves(bias_up)[0])
    active_low = gelu_value.astype(BF16)
    resid_two = hidden_one + own_tokens(contract_last(active_low, half_down))
    layer_val, normed_two, inv_two = layer_norm(resid_two + bias_down, gain_two, shift_two)
    layer_out = layer_val.astype(BF16)

    grad_y = cotangent.astype(F32)
    grad_gain_two = jnp.sum(grad_y * normed_two, 0)
    grad_shift_two = jnp.sum(grad_y, 0)
    grad_resid_two = norm_back(grad_y, normed_two, inv_two, gain_two)
    grad_low_two = pair(grad_resid_two.astype(BF16))
    grad_bias_down = jnp.sum(grad_resid_two, 0)
    sum_down = contract_first(grad_low_two, active_low).astype(BF16)
    sum_down = over_plane(sum_down)
    grad_inner = dot(grad_low_two, half_down) * gelu_slope
    grad_inner_low = grad_inner.astype(BF16)
    grad_bias_up = jnp.sum(grad_inner, 0)
    grad_hidden = grad_resid_two + own_tokens(contract_last(grad_inner_low, half_up))
    sum_up = contract_first(hidden_two, grad_inner_low).astype(BF16)
    sum_up = over_plane(after(sum_up, sum_down))
    grad_gain_one = jnp.sum(grad_hidden * normed_one, 0)
    grad_shift_one = jnp.sum(grad_hidden, 0)
    grad_resid_one = norm_back(grad_hidden, normed_one, inv_one, gain_one)
    grad_low_one = grad_resid_one.astype(BF16)
    grad_bias_out = jnp.sum(grad_resid_one, 0)
    grad_kept, grad_sent = halves(grad_low_one)
    grad_attn = (
        contract_last(grad_kept, half_out) + contract_last(grad_sent, other_out)
    ).astype(BF16)
    grad_attn_cols = lax.all_to_all(grad_attn, "seq", split_axis=1, concat_axis=0, tiled=True)
    grad_out_two = jnp.concatenate([grad_kept, swap(grad_sent)], 0)
    sum_out = contract_first(pair(attn_tok), grad_out_two).astype(BF16)
    sum_out = over_plane(after(sum_out, sum_up))

    grad_own = attend_backward(projected, outputs, log_total, grad_attn_cols)
    grad_tok = lax.all_to_all(grad_own, "seq", split_axis=0, concat_axis=1, tiled=True)
    own_kept, own_sent = halves(grad_own)
    other_sum = swap(contract_first(seq_hidden, own_sent).astype(BF16))
    sum_qkv = (contract_first(seq_hidden, own_kept) + other_sum.astype(F32)).astype(BF16)
    sum_qkv = over_plane(sum_qkv)
    to_core = pick(sum_qkv, nc - 1 - core_at, 0)
    sum_qkv = in_order(
        pick(sum_qkv, core_at, 0), [swap(to_core)], "core", nc, 1
    ).reshape(ns, rows, 3 * own)
    sum_qkv = in_order(
        pick(sum_qkv, seq_at, 0),
        [
            shift(pick(sum_qkv, lax.rem(seq_at + ns - d, ns), 0), "seq", ns, ns - d)
            for d in range(1, ns)
        ],
        "seq", ns, 0,
    )
    sum_qkv = sum_qkv.astype(F32).reshape(ns, rows, 3, own).transpose(1, 2, 0, 3)
    sum_qkv = sum_qkv.reshape(rows, 3 * width)
    tok_kept, tok_other = halves(grad_tok)
    grad_input = (
        grad_resid_one + contract_last(tok_kept, half_qkv) + contract_last(tok_other, other_qkv)
    )
    sum_down = over_line(after(sum_down, grad_attn_cols))
    sum_up = over_line(sum_up)
    sum_out = over_line(sum_out)

    def spread(part, whole, start):
        return lax.dynamic_update_slice_in_dim(jnp.zeros((whole,), F32), part, start, 0)

    own_sums = jnp.sum(grad_own.astype(F32), 0)

    def sum_small(parts):
        stacked = jnp.concatenate([part.reshape(devices, -1) for part in parts], 1)
        arrived = lax.all_to_all(stacked, ALL, split_axis=0, concat_axis=0, tiled=True)
        total = jnp.sum(arrived, 0)
        ends, place = [], 0
        for part in parts:
            count = part.shape[0] // devices
            ends.append(total[place : place + count])
            place += count
        return ends

    (sum_gain_two, sum_shift_two, sum_bias_down, sum_bias_up, sum_gain_one, sum_shift_one,
     sum_bias_out) = sum_small(
        (grad_gain_two, grad_shift_two, grad_bias_down,
         spread(grad_bias_up, inner_width, core_at * half), grad_gain_one, grad_shift_one,
         grad_bias_out)
    )
    sum_bias_query, sum_bias_value = sum_small(
        (spread(own_sums[:own], width, seq_at * own),
         spread(own_sums[2 * own :], width, seq_at * own))
    )
    return (layer_out, grad_input, sum_qkv, sum_bias_query, sum_bias_value, sum_out, sum_bias_out,
            sum_gain_one, sum_shift_one, sum_up, sum_bias_up, sum_down, sum_bias_down,
            sum_gain_two, sum_shift_two)


def solution(mesh):
    dp, ns = mesh.shape["dp"], mesh.shape["seq"]
    nc = 2
    ny = 2 if (dp // nc) % 2 == 0 else 1
    sizes = (ny, dp // (nc * ny), nc, ns)
    fine = Mesh(mesh.devices.reshape(sizes), ALL)
    matrix, vector = P(ALL, None), P(ALL)
    in_specs = (matrix, matrix, matrix, vector, vector, matrix, vector, vector, vector, matrix,
                vector, matrix, vector, vector, vector)
    out_specs = (matrix, matrix, matrix, vector, vector, matrix, vector, vector, vector, matrix,
                 vector, matrix, vector, vector, vector)

    def on_device(*args):
        return body(sizes, *args)

    return jax.shard_map(
        on_device, mesh=fine, in_specs=in_specs, out_specs=out_specs, check_vma=False
    )
```

```python
import functools
import math

import jax
import jax.numpy as jnp
from jax import lax
from jax.experimental import pallas as pl
from jax.experimental.pallas import tpu as pltpu
from jax.sharding import Mesh
from jax.sharding import PartitionSpec as P


HD = 64
EPS = 1e-12
ALL = ("y", "x", "core", "seq")
BF16 = jnp.bfloat16
F32 = jnp.float32


def layer_norm(residual, gain_vec, shift_vec):
    row_mean = jnp.mean(residual, -1, keepdims=True)
    centred = residual - row_mean
    variance = jnp.mean(centred * centred, -1, keepdims=True)
    inv_std = lax.rsqrt(variance + EPS)
    normed = centred * inv_std
    return (normed * gain_vec + shift_vec, normed, inv_std)


def norm_back(incoming, normed, inv_std, gain_vec):
    scaled = incoming * gain_vec
    return inv_std * (
        scaled
        - jnp.mean(scaled, -1, keepdims=True)
        - normed * jnp.mean(scaled * normed, -1, keepdims=True)
    )


def gelu_both(inner):
    normal_cdf = 0.5 * (1.0 + jax.scipy.special.erf(inner / math.sqrt(2.0)))
    gelu_value = inner * normal_cdf
    gelu_slope = normal_cdf + inner * jnp.exp(-0.5 * inner * inner) / math.sqrt(2.0 * math.pi)
    return (gelu_value, gelu_slope)


def dot(left, right):
    return jnp.dot(left, right, preferred_element_type=F32)


def contract_last(left, right):
    return lax.dot_general(left, right, (((1,), (1,)), ((), ())), preferred_element_type=F32)


def contract_first(left, right):
    return lax.dot_general(left, right, (((0,), (0,)), ((), ())), preferred_element_type=F32)


def lanes_of(head, shape):
    lane = lax.broadcasted_iota(jnp.int32, shape, len(shape) - 1)
    return (lane >= head * HD) & (lane < (head + 1) * HD)


def forward_kernel(score_scale, query_ref, key_ref, value_ref, out_ref, total_ref, value_t, out_t):
    head = pl.program_id(1)

    @pl.when((pl.program_id(0) == 0) & (head == 0))
    def _():
        value_t[...] = value_ref[...].astype(F32).T.astype(BF16)

    query = query_ref[...]
    query = jnp.where(lanes_of(head, query.shape), query, jnp.zeros_like(query))
    scores = contract_last(key_ref[...], query) * score_scale
    top = jnp.max(scores, 0, keepdims=True)
    weights = jnp.exp(scores - top)
    total = jnp.sum(weights, 0, keepdims=True)
    total_ref[pl.ds(head, 1), :] = top + jnp.log(total)
    probs = (weights * (1.0 / total)).astype(BF16)
    rows = pl.ds(pl.multiple_of(head * HD, HD), HD)
    out_t[rows, :] = dot(value_t[rows, :], probs)

    @pl.when(head == pl.num_programs(1) - 1)
    def _():
        out_ref[...] = out_t[...].T.astype(BF16)


def attend_forward(projected):
    length, width = projected.shape[0], projected.shape[1] // 3
    block = min(256, length)
    heads = width // HD
    return pl.pallas_call(
        functools.partial(forward_kernel, 1.0 / math.sqrt(HD)),
        grid=(length // block, heads),
        in_specs=[
            pl.BlockSpec((block, width), lambda i, h: (i, 0)),
            pl.BlockSpec((length, width), lambda i, h: (0, 1)),
            pl.BlockSpec((length, width), lambda i, h: (0, 2)),
        ],
        out_specs=[
            pl.BlockSpec((block, width), lambda i, h: (i, 0)),
            pl.BlockSpec((heads, block), lambda i, h: (0, i)),
        ],
        out_shape=[
            jax.ShapeDtypeStruct((length, width), BF16),
            jax.ShapeDtypeStruct((heads, length), F32),
        ],
        scratch_shapes=[pltpu.VMEM((width, length), BF16), pltpu.VMEM((width, block), F32)],
        compiler_params=pltpu.CompilerParams(vmem_limit_bytes=24 * 2**20),
        cost_estimate=pl.CostEstimate(
            flops=4 * length * length * width,
            bytes_accessed=8 * length * width,
            transcendentals=heads * length * length,
        ),
        name="attend_forward",
    )(projected, projected, projected)


def backward_kernel(score_scale, block, query_ref, key_ref, value_ref, out_ref, total_ref,
                    grad_ref, result_ref, key_t, delta, query_t):
    step, head = pl.program_id(0), pl.program_id(1)
    width = query_ref.shape[1]
    heads = width // HD
    blocks = key_t.shape[0]

    @pl.when((step == 0) & (head == 0))
    def _():
        for number in range(blocks):
            key_t[number] = key_ref[pl.ds(number * block, block), :].astype(F32).T.astype(BF16)
        product = (grad_ref[...].astype(F32) * out_ref[...].astype(F32)).T
        for number in range(heads):
            delta[pl.ds(number, 1), :] = jnp.sum(
                product[number * HD : (number + 1) * HD], 0, keepdims=True
            )

    here = pl.ds(pl.multiple_of(step * block, block), block)
    mask = lanes_of(head, (block, width))
    key, value = key_ref[here, :], value_ref[here, :]
    key = jnp.where(mask, key, jnp.zeros_like(key))
    value = jnp.where(mask, value, jnp.zeros_like(value))
    scores = contract_last(key, query_ref[...]) * score_scale
    probs = jnp.exp(scores - total_ref[pl.ds(head, 1), :])
    grad_value = dot(probs.astype(BF16), grad_ref[...])
    grad_probs = contract_last(value, grad_ref[...])
    grad_scores = (probs * (grad_probs - delta[pl.ds(head, 1), :])).astype(BF16)
    grad_key = dot(grad_scores, query_ref[...]) * score_scale
    rows = pl.ds(pl.multiple_of(head * HD, HD), HD)
    part = dot(key_t[step, rows, :], grad_scores)

    @pl.when(step == 0)
    def _():
        query_t[rows, :] = part

    @pl.when(step > 0)
    def _():
        query_t[rows, :] += part

    for place, piece in ((width, grad_key), (2 * width, grad_value)):
        low = piece.astype(BF16)
        held = result_ref[here, place : place + width]
        result_ref[here, place : place + width] = jnp.where(mask, low, held)

    @pl.when((step == pl.num_programs(0) - 1) & (head == heads - 1))
    def _():
        result_ref[:, :width] = (query_t[...] * score_scale).T.astype(BF16)


def attend_backward(projected, outputs, log_total, grad_out):
    length, width = outputs.shape
    block = min(256, length)
    heads = width // HD
    full = pl.BlockSpec((length, width), lambda i, h: (0, 0))
    return pl.pallas_call(
        functools.partial(backward_kernel, 1.0 / math.sqrt(HD), block),
        grid=(length // block, heads),
        in_specs=[
            full,
            pl.BlockSpec((length, width), lambda i, h: (0, 1)),
            pl.BlockSpec((length, width), lambda i, h: (0, 2)),
            full,
            pl.BlockSpec((heads, length), lambda i, h: (0, 0)),
            full,
        ],
        out_specs=pl.BlockSpec((length, 3 * width), lambda i, h: (0, 0)),
        out_shape=jax.ShapeDtypeStruct((length, 3 * width), BF16),
        scratch_shapes=[
            pltpu.VMEM((length // block, width, block), BF16),
            pltpu.VMEM((heads, length), F32),
            pltpu.VMEM((width, length), F32),
        ],
        compiler_params=pltpu.CompilerParams(vmem_limit_bytes=32 * 2**20),
        cost_estimate=pl.CostEstimate(
            flops=10 * length * length * width,
            bytes_accessed=16 * length * width,
            transcendentals=heads * length * length,
        ),
        name="attend_backward",
    )(projected, projected, projected, outputs, log_total, grad_out)


def shift(block, axis, size, distance):
    return lax.ppermute(block, axis, [(i, (i + distance) % size) for i in range(size)])


def after(value, *earlier):
    return lax.optimization_barrier((value,) + earlier)[0]


def shifts(block, axis, size):
    return [shift(block, axis, size, size - d) for d in range(1, size)]


def relayed(block, axis, size):
    me = lax.axis_index(axis)
    up, down = [block], [block]
    for step in range(1, size):
        up.append(lax.ppermute(up[-1], axis, [(i, i + 1) for i in range(step - 1, size - 1)]))
        down.append(lax.ppermute(down[-1], axis, [(i, i - 1) for i in range(1, size - step + 1)]))
    return [jnp.where(me + d < size, down[d], up[size - d]) for d in range(1, size)]


def ordered(block, others, axis, size):
    if size == 1:
        return [block]
    ahead = [block] + list(others)
    me = lax.axis_index(axis)
    if size == 2:
        return [jnp.where(me == 0, *ahead), jnp.where(me == 0, *ahead[::-1])]
    return [
        lax.select_n(me, *[ahead[(place - at) % size] for at in range(size)])
        for place in range(size)
    ]


def in_order(block, others, axis, size, dim):
    return jnp.stack(ordered(block, others, axis, size), dim)


def gather_blocks(block, axis, size, dim):
    return in_order(block, shifts(block, axis, size), axis, size, dim)


def pick(blocks, index, dim):
    if blocks.shape[dim] == 2:
        first = lax.index_in_dim(blocks, 0, dim, keepdims=False)
        second = lax.index_in_dim(blocks, 1, dim, keepdims=False)
        return jnp.where(index == 0, first, second)
    return lax.dynamic_index_in_dim(blocks, index, dim, keepdims=False)


def reduce_blocks(blocks, axis, size, dim):
    me = lax.axis_index(axis)
    total = pick(blocks, me, dim).astype(F32)
    for distance in range(1, size):
        sent = pick(blocks, lax.rem(me + distance, size), dim).astype(BF16)
        total = total + shift(sent, axis, size, distance).astype(F32)
    return total


def body(sizes, hidden_states, cotangent, w_qkv, b_query, b_value, w_out, b_out, ln1_gain,
         ln1_shift, w_up, b_up, w_down, b_down, ln2_gain, ln2_shift):
    ny, nx, nc, ns = sizes
    devices = ny * nx * nc * ns
    rows, width = w_out.shape
    tokens = hidden_states.shape[0]
    inner_width = w_up.shape[1]
    own = width // ns
    seq_at = lax.axis_index("seq")
    core_at = lax.axis_index("core")

    def halves(matrix):
        half = matrix.shape[-1] // nc
        parts = matrix.reshape(matrix.shape[:-1] + (nc, half))
        return pick(parts, core_at, parts.ndim - 2), pick(parts, nc - 1 - core_at, parts.ndim - 2)

    def swap(block):
        return shift(block, "core", nc, 1)

    def pair(block):
        return jnp.concatenate([block, swap(block)], 0)

    def own_tokens(part):
        return part[:tokens] + swap(part[tokens:])

    def own_columns(shard):
        kept, sent = halves(shard)
        return in_order(kept, [swap(sent)], "core", nc, 0)

    def line_of(block, others):
        line = in_order(block, others, "seq", ns, 1)
        return line.reshape(block.shape[0], ns * block.shape[1], block.shape[2])

    def plane_of(line):
        low_x = shifts(line[0], "x", nx)
        high_y = shifts(line[1], "y", ny)
        low = in_order(line[0], low_x, "x", nx, 0)
        high = in_order(line[1], high_y, "y", ny, 0)
        low_y = shifts(low, "y", ny)
        high_x = shifts(high, "x", nx)
        low = in_order(low, low_y, "y", ny, 0)
        high = in_order(high, high_x, "x", nx, 1)
        return jnp.stack([low, high], 2).reshape(ny * nx * nc * line.shape[1], line.shape[2])

    def over_plane(full):
        line_rows = full.shape[0] // (ny * nx * nc)
        parts = full.reshape(ny, nx, nc, line_rows, full.shape[1])
        low = reduce_blocks(parts[:, :, 0], "x", nx, 1).astype(BF16)
        high = reduce_blocks(parts[:, :, 1], "y", ny, 0).astype(BF16)
        low = reduce_blocks(low, "y", ny, 0).astype(BF16)
        high = reduce_blocks(high, "x", nx, 0).astype(BF16)
        return jnp.stack([low, high], 0)

    def over_line(part):
        blocks = part.reshape(nc, ns, part.shape[1] // ns, part.shape[2])
        total = reduce_blocks(blocks, "seq", ns, 1)
        kept = pick(total, core_at, 0)
        came = swap(pick(total, nc - 1 - core_at, 0).astype(BF16)).astype(F32)
        low = jnp.where(core_at == 0, kept, came)
        high = jnp.where(core_at == 0, came, kept)
        return jnp.concatenate([low, high], 1)

    def to_owners(matrix, kept, count):
        came = [
            shift(matrix[d * count : (d + 1) * count], "seq", ns, d) for d in range(1, ns)
        ]
        return jnp.concatenate(ordered(kept, came[::-1], "seq", ns), 1)

    def to_heads(matrix):
        columns = matrix.shape[1] // ns

        def block(d):
            return lax.dynamic_slice_in_dim(
                matrix, lax.rem(seq_at + d, ns) * columns, columns, 1
            )

        sent = [block(d) for d in range(1, ns)]
        came = [shift(part, "seq", ns, d) for d, part in enumerate(sent, 1)]
        return jnp.concatenate([block(0)] + came[::-1], 0)

    by_owner = w_qkv.reshape(rows, 3, ns, own).transpose(0, 2, 1, 3).reshape(rows, 3 * width)
    to_owner = by_owner.reshape(rows, ns, 3 * own)
    kept = lax.dynamic_index_in_dim(to_owner, seq_at, 1, keepdims=False)
    came = [
        shift(
            lax.dynamic_index_in_dim(to_owner, lax.rem(seq_at + ns - d, ns), 1, keepdims=False),
            "seq", ns, ns - d,
        )
        for d in range(1, ns)
    ]
    own_line = in_order(kept, came, "seq", ns, 0).reshape(ns * rows, 3 * own)
    plane = gather_blocks(gather_blocks(own_line, "x", nx, 0), "y", ny, 0)
    own_qkv = gather_blocks(plane, "core", nc, 2).reshape(width, 3 * own)

    small = (b_query, b_value, b_out, ln1_gain, ln1_shift, b_up, b_down, ln2_gain, ln2_shift)
    packed = jnp.concatenate((after(small[0], *came),) + small[1:])[None]
    packed = lax.all_to_all(
        jnp.tile(packed, (devices, 1)), ALL, split_axis=0, concat_axis=0, tiled=True
    ).astype(F32)
    vectors, place = [], 0
    for shard in small:
        vectors.append(packed[:, place : place + shard.shape[0]].reshape(-1))
        place += shard.shape[0]
    (bias_query, bias_value, bias_out, gain_one, shift_one, bias_up, bias_down, gain_two,
     shift_two) = vectors

    up_out = own_columns(w_up), own_columns(w_out)
    up_out = after(jnp.concatenate(up_out, 2), *came)
    up_line = shifts(up_out, "seq", ns)
    hidden_sent = after(hidden_states, *up_line)
    hidden_line = relayed(hidden_sent, "seq", ns)
    seq_hidden = jnp.concatenate([hidden_sent] + hidden_line, 0)
    down_own = after(own_columns(w_down), *hidden_line)
    down_line = shifts(down_own, "seq", ns)
    half_up_out = plane_of(line_of(up_out, up_line))
    half = inner_width // nc
    half_up, half_out = half_up_out[:, :half], half_up_out[:, half:]
    other_out = swap(half_out)
    half_down = plane_of(line_of(down_own, down_line))

    own_bias = jnp.concatenate(
        [
            lax.dynamic_slice_in_dim(bias_query, seq_at * own, own),
            jnp.zeros((own,), F32),
            lax.dynamic_slice_in_dim(bias_value, seq_at * own, own),
        ]
    )
    projected = (dot(seq_hidden, own_qkv) + own_bias).astype(BF16)
    outputs, log_total = attend_forward(projected)
    attn_tok = to_owners(outputs, outputs[:tokens], tokens)
    qkv_own = after(own_columns(by_owner), attn_tok)
    qkv_line = shifts(qkv_own, "seq", ns)
    half_qkv = plane_of(after(line_of(qkv_own, qkv_line), half_down))
    other_qkv = swap(half_qkv)

    mixed, mixed_other = dot(attn_tok, half_out), dot(attn_tok, other_out)
    mixed = jnp.concatenate(
        [
            jnp.where(core_at == 0, mixed, mixed_other),
            jnp.where(core_at == 0, mixed_other, mixed),
        ],
        1,
    )
    resid_one = hidden_states.astype(F32) + mixed + bias_out
    hidden_one, normed_one, inv_one = layer_norm(resid_one, gain_one, shift_one)
    hidden_low = hidden_one.astype(BF16)

    hidden_two = pair(hidden_low)
    inner = dot(hidden_two, half_up)
    gelu_value, gelu_slope = gelu_both(inner + halves(bias_up)[0])
    active_low = gelu_value.astype(BF16)
    resid_two = hidden_one + own_tokens(contract_last(active_low, half_down))
    layer_val, normed_two, inv_two = layer_norm(resid_two + bias_down, gain_two, shift_two)
    layer_out = layer_val.astype(BF16)

    grad_y = cotangent.astype(F32)
    grad_gain_two = jnp.sum(grad_y * normed_two, 0)
    grad_shift_two = jnp.sum(grad_y, 0)
    grad_resid_two = norm_back(grad_y, normed_two, inv_two, gain_two)
    grad_low_two = pair(grad_resid_two.astype(BF16))
    grad_bias_down = jnp.sum(grad_resid_two, 0)
    sum_down = contract_first(grad_low_two, active_low).astype(BF16)
    sum_down = over_plane(sum_down)
    grad_inner = dot(grad_low_two, half_down)
    grad_inner = grad_inner * gelu_slope
    grad_inner_low = grad_inner.astype(BF16)
    grad_bias_up = jnp.sum(grad_inner, 0)
    grad_hidden = grad_resid_two + own_tokens(contract_last(grad_inner_low, half_up))
    sum_up = contract_first(hidden_two, grad_inner_low).astype(BF16)
    sum_up = over_plane(sum_up)
    grad_gain_one = jnp.sum(grad_hidden * normed_one, 0)
    grad_shift_one = jnp.sum(grad_hidden, 0)
    grad_resid_one = norm_back(grad_hidden, normed_one, inv_one, gain_one)
    grad_low_one = grad_resid_one.astype(BF16)
    grad_bias_out = jnp.sum(grad_resid_one, 0)
    grad_kept, grad_sent = halves(grad_low_one)
    grad_attn = (
        contract_last(grad_kept, half_out) + contract_last(grad_sent, other_out)
    ).astype(BF16)
    grad_attn_cols = to_heads(grad_attn)
    grad_out_two = jnp.concatenate([grad_kept, swap(grad_sent)], 0)
    sum_out = contract_first(pair(attn_tok), grad_out_two).astype(BF16)
    sum_out = over_plane(sum_out)

    grad_own = attend_backward(projected, outputs, log_total, grad_attn_cols)
    grad_tok = to_owners(grad_own, grad_own[:tokens], tokens)
    own_kept, own_sent = halves(grad_own)
    other_sum = swap(contract_first(seq_hidden, own_sent).astype(BF16))
    sum_qkv = (contract_first(seq_hidden, own_kept) + other_sum.astype(F32)).astype(BF16)
    sum_qkv = over_plane(sum_qkv)
    to_core = pick(sum_qkv, nc - 1 - core_at, 0)
    sum_qkv = in_order(
        pick(sum_qkv, core_at, 0), [swap(to_core)], "core", nc, 1
    ).reshape(ns, rows, 3 * own)
    sum_qkv = in_order(
        pick(sum_qkv, seq_at, 0),
        [
            shift(pick(sum_qkv, lax.rem(seq_at + ns - d, ns), 0), "seq", ns, ns - d)
            for d in range(1, ns)
        ],
        "seq", ns, 0,
    )
    sum_qkv = sum_qkv.astype(F32).reshape(ns, rows, 3, own).transpose(1, 2, 0, 3)
    sum_qkv = sum_qkv.reshape(rows, 3 * width)
    tok_kept, tok_other = halves(grad_tok)
    grad_input = (
        grad_resid_one
        + contract_last(tok_kept, half_qkv)
        + contract_last(tok_other, other_qkv)
    )
    sum_down = over_line(after(sum_down, grad_attn_cols))
    sum_up = over_line(sum_up)
    sum_out = over_line(sum_out)

    def spread(part, whole, start):
        return lax.dynamic_update_slice_in_dim(jnp.zeros((whole,), F32), part, start, 0)

    own_sums = jnp.sum(grad_own.astype(F32), 0)

    def sum_small(parts):
        stacked = jnp.concatenate([part.reshape(devices, -1) for part in parts], 1)
        arrived = lax.all_to_all(after(stacked, grad_tok), ALL, split_axis=0, concat_axis=0, tiled=True)
        total = jnp.sum(arrived, 0)
        ends, place = [], 0
        for part in parts:
            count = part.shape[0] // devices
            ends.append(total[place : place + count])
            place += count
        return ends

    (sum_gain_two, sum_shift_two, sum_bias_down, sum_bias_up, sum_gain_one, sum_shift_one,
     sum_bias_out, sum_bias_query, sum_bias_value) = sum_small(
        (grad_gain_two, grad_shift_two, grad_bias_down,
         spread(grad_bias_up, inner_width, core_at * half), grad_gain_one, grad_shift_one,
         grad_bias_out, spread(own_sums[:own], width, seq_at * own),
         spread(own_sums[2 * own :], width, seq_at * own))
    )
    return (layer_out, grad_input, sum_qkv, sum_bias_query, sum_bias_value, sum_out, sum_bias_out,
            sum_gain_one, sum_shift_one, sum_up, sum_bias_up, sum_down, sum_bias_down,
            sum_gain_two, sum_shift_two)


def solution(mesh):
    dp, ns = mesh.shape["dp"], mesh.shape["seq"]
    nc = 2
    ny = 2 if (dp // nc) % 2 == 0 else 1
    sizes = (ny, dp // (nc * ny), nc, ns)
    fine = Mesh(mesh.devices.reshape(sizes), ALL)
    matrix, vector = P(ALL, None), P(ALL)
    in_specs = (matrix, matrix, matrix, vector, vector, matrix, vector, vector, vector, matrix,
                vector, matrix, vector, vector, vector)
    out_specs = (matrix, matrix, matrix, vector, vector, matrix, vector, vector, vector, matrix,
                 vector, matrix, vector, vector, vector)

    def on_device(*args):
        return body(sizes, *args)

    return jax.shard_map(
        on_device, mesh=fine, in_specs=in_specs, out_specs=out_specs, check_vma=False
    )
```

```python
import functools
import math

import jax
import jax.numpy as jnp
from jax import lax
from jax.experimental import pallas as pl
from jax.experimental.pallas import tpu as pltpu
from jax.sharding import Mesh
from jax.sharding import PartitionSpec as P


HD = 64
EPS = 1e-12
ALL = ("y", "x", "core", "seq")
BF16 = jnp.bfloat16
F32 = jnp.float32


def layer_norm(residual, gain_vec, shift_vec):
    row_mean = jnp.mean(residual, -1, keepdims=True)
    centred = residual - row_mean
    variance = jnp.mean(centred * centred, -1, keepdims=True)
    inv_std = lax.rsqrt(variance + EPS)
    normed = centred * inv_std
    return (normed * gain_vec + shift_vec, normed, inv_std)


def norm_back(incoming, normed, inv_std, gain_vec):
    scaled = incoming * gain_vec
    return inv_std * (
        scaled
        - jnp.mean(scaled, -1, keepdims=True)
        - normed * jnp.mean(scaled * normed, -1, keepdims=True)
    )


def gelu_both(inner):
    normal_cdf = 0.5 * (1.0 + jax.scipy.special.erf(inner / math.sqrt(2.0)))
    gelu_value = inner * normal_cdf
    gelu_slope = normal_cdf + inner * jnp.exp(-0.5 * inner * inner) / math.sqrt(2.0 * math.pi)
    return (gelu_value, gelu_slope)


def dot(left, right):
    return jnp.dot(left, right, preferred_element_type=F32)


def contract_last(left, right):
    return lax.dot_general(left, right, (((1,), (1,)), ((), ())), preferred_element_type=F32)


def contract_first(left, right):
    return lax.dot_general(left, right, (((0,), (0,)), ((), ())), preferred_element_type=F32)


def lanes_of(head, shape):
    lane = lax.broadcasted_iota(jnp.int32, shape, len(shape) - 1)
    return (lane >= head * HD) & (lane < (head + 1) * HD)


def forward_kernel(score_scale, query_ref, key_ref, value_ref, out_ref, total_ref, value_t, out_t):
    head = pl.program_id(1)

    @pl.when((pl.program_id(0) == 0) & (head == 0))
    def _():
        value_t[...] = value_ref[...].astype(F32).T.astype(BF16)

    query = query_ref[...]
    query = jnp.where(lanes_of(head, query.shape), query, jnp.zeros_like(query))
    scores = contract_last(key_ref[...], query) * score_scale
    top = jnp.max(scores, 0, keepdims=True)
    weights = jnp.exp(scores - top)
    total = jnp.sum(weights, 0, keepdims=True)
    total_ref[pl.ds(head, 1), :] = top + jnp.log(total)
    probs = (weights * (1.0 / total)).astype(BF16)
    rows = pl.ds(pl.multiple_of(head * HD, HD), HD)
    out_t[rows, :] = dot(value_t[rows, :], probs)

    @pl.when(head == pl.num_programs(1) - 1)
    def _():
        out_ref[...] = out_t[...].T.astype(BF16)


def attend_forward(projected):
    length, width = projected.shape[0], projected.shape[1] // 3
    block = min(512, length)
    heads = width // HD
    return pl.pallas_call(
        functools.partial(forward_kernel, 1.0 / math.sqrt(HD)),
        grid=(length // block, heads),
        in_specs=[
            pl.BlockSpec((block, width), lambda i, h: (i, 0)),
            pl.BlockSpec((length, width), lambda i, h: (0, 1)),
            pl.BlockSpec((length, width), lambda i, h: (0, 2)),
        ],
        out_specs=[
            pl.BlockSpec((block, width), lambda i, h: (i, 0)),
            pl.BlockSpec((heads, block), lambda i, h: (0, i)),
        ],
        out_shape=[
            jax.ShapeDtypeStruct((length, width), BF16),
            jax.ShapeDtypeStruct((heads, length), F32),
        ],
        scratch_shapes=[pltpu.VMEM((width, length), BF16), pltpu.VMEM((width, block), F32)],
        compiler_params=pltpu.CompilerParams(vmem_limit_bytes=24 * 2**20),
        cost_estimate=pl.CostEstimate(
            flops=4 * length * length * width,
            bytes_accessed=8 * length * width,
            transcendentals=heads * length * length,
        ),
        name="attend_forward",
    )(projected, projected, projected)


def backward_kernel(score_scale, block, query_ref, key_ref, value_ref, out_ref, total_ref,
                    grad_ref, result_ref, key_t, delta, query_t):
    step, head = pl.program_id(0), pl.program_id(1)
    width = query_ref.shape[1]
    heads = width // HD
    blocks = key_t.shape[0]

    @pl.when((step == 0) & (head == 0))
    def _():
        for number in range(blocks):
            key_t[number] = key_ref[pl.ds(number * block, block), :].astype(F32).T.astype(BF16)
        product = (grad_ref[...].astype(F32) * out_ref[...].astype(F32)).T
        for number in range(heads):
            delta[pl.ds(number, 1), :] = jnp.sum(
                product[number * HD : (number + 1) * HD], 0, keepdims=True
            )

    here = pl.ds(pl.multiple_of(step * block, block), block)
    mask = lanes_of(head, (block, width))
    key, value = key_ref[here, :], value_ref[here, :]
    key = jnp.where(mask, key, jnp.zeros_like(key))
    value = jnp.where(mask, value, jnp.zeros_like(value))
    scores = contract_last(key, query_ref[...]) * score_scale
    probs = jnp.exp(scores - total_ref[pl.ds(head, 1), :])
    grad_value = dot(probs.astype(BF16), grad_ref[...])
    grad_probs = contract_last(value, grad_ref[...])
    grad_scores = (probs * (grad_probs - delta[pl.ds(head, 1), :])).astype(BF16)
    grad_key = dot(grad_scores, query_ref[...]) * score_scale
    rows = pl.ds(pl.multiple_of(head * HD, HD), HD)
    part = dot(key_t[step, rows, :], grad_scores)

    @pl.when(step == 0)
    def _():
        query_t[rows, :] = part

    @pl.when(step > 0)
    def _():
        query_t[rows, :] += part

    for place, piece in ((width, grad_key), (2 * width, grad_value)):
        low = piece.astype(BF16)
        held = result_ref[here, place : place + width]
        result_ref[here, place : place + width] = jnp.where(mask, low, held)

    @pl.when((step == pl.num_programs(0) - 1) & (head == heads - 1))
    def _():
        result_ref[:, :width] = (query_t[...] * score_scale).T.astype(BF16)


def attend_backward(projected, outputs, log_total, grad_out):
    length, width = outputs.shape
    block = min(512, length)
    heads = width // HD
    full = pl.BlockSpec((length, width), lambda i, h: (0, 0))
    return pl.pallas_call(
        functools.partial(backward_kernel, 1.0 / math.sqrt(HD), block),
        grid=(length // block, heads),
        in_specs=[
            full,
            pl.BlockSpec((length, width), lambda i, h: (0, 1)),
            pl.BlockSpec((length, width), lambda i, h: (0, 2)),
            full,
            pl.BlockSpec((heads, length), lambda i, h: (0, 0)),
            full,
        ],
        out_specs=pl.BlockSpec((length, 3 * width), lambda i, h: (0, 0)),
        out_shape=jax.ShapeDtypeStruct((length, 3 * width), BF16),
        scratch_shapes=[
            pltpu.VMEM((length // block, width, block), BF16),
            pltpu.VMEM((heads, length), F32),
            pltpu.VMEM((width, length), F32),
        ],
        compiler_params=pltpu.CompilerParams(vmem_limit_bytes=32 * 2**20),
        cost_estimate=pl.CostEstimate(
            flops=10 * length * length * width,
            bytes_accessed=16 * length * width,
            transcendentals=heads * length * length,
        ),
        name="attend_backward",
    )(projected, projected, projected, outputs, log_total, grad_out)


def shift(block, axis, size, distance):
    return lax.ppermute(block, axis, [(i, (i + distance) % size) for i in range(size)])


def after(value, *earlier):
    return lax.optimization_barrier((value,) + earlier)[0]


def shifts(block, axis, size):
    return [shift(block, axis, size, size - d) for d in range(1, size)]


def relayed(block, axis, size):
    me = lax.axis_index(axis)
    up, down = [block], [block]
    for step in range(1, size):
        up.append(lax.ppermute(up[-1], axis, [(i, i + 1) for i in range(step - 1, size - 1)]))
        down.append(lax.ppermute(down[-1], axis, [(i, i - 1) for i in range(1, size - step + 1)]))
    return [jnp.where(me + d < size, down[d], up[size - d]) for d in range(1, size)]


def ordered(block, others, axis, size):
    if size == 1:
        return [block]
    ahead = [block] + list(others)
    me = lax.axis_index(axis)
    if size == 2:
        return [jnp.where(me == 0, *ahead), jnp.where(me == 0, *ahead[::-1])]
    return [
        lax.select_n(me, *[ahead[(place - at) % size] for at in range(size)])
        for place in range(size)
    ]


def in_order(block, others, axis, size, dim):
    return jnp.stack(ordered(block, others, axis, size), dim)


def gather_blocks(block, axis, size, dim):
    return in_order(block, shifts(block, axis, size), axis, size, dim)


def pick(blocks, index, dim):
    if blocks.shape[dim] == 2:
        first = lax.index_in_dim(blocks, 0, dim, keepdims=False)
        second = lax.index_in_dim(blocks, 1, dim, keepdims=False)
        return jnp.where(index == 0, first, second)
    return lax.dynamic_index_in_dim(blocks, index, dim, keepdims=False)


def reduce_blocks(blocks, axis, size, dim):
    me = lax.axis_index(axis)
    total = pick(blocks, me, dim).astype(F32)
    for distance in range(1, size):
        sent = pick(blocks, lax.rem(me + distance, size), dim).astype(BF16)
        total = total + shift(sent, axis, size, distance).astype(F32)
    return total


def body(sizes, hidden_states, cotangent, w_qkv, b_query, b_value, w_out, b_out, ln1_gain,
         ln1_shift, w_up, b_up, w_down, b_down, ln2_gain, ln2_shift):
    ny, nx, nc, ns = sizes
    devices = ny * nx * nc * ns
    rows, width = w_out.shape
    tokens = hidden_states.shape[0]
    inner_width = w_up.shape[1]
    own = width // ns
    seq_at = lax.axis_index("seq")
    core_at = lax.axis_index("core")

    def halves(matrix):
        half = matrix.shape[-1] // nc
        parts = matrix.reshape(matrix.shape[:-1] + (nc, half))
        return pick(parts, core_at, parts.ndim - 2), pick(parts, nc - 1 - core_at, parts.ndim - 2)

    def swap(block):
        return shift(block, "core", nc, 1)

    def pair(block):
        return jnp.concatenate([block, swap(block)], 0)

    def own_tokens(part):
        return part[:tokens] + swap(part[tokens:])

    def own_columns(shard):
        kept, sent = halves(shard)
        return in_order(kept, [swap(sent)], "core", nc, 0)

    def line_of(block, others):
        line = in_order(block, others, "seq", ns, 1)
        return line.reshape(block.shape[0], ns * block.shape[1], block.shape[2])

    def plane_of(line):
        low_x = shifts(line[0], "x", nx)
        high_y = shifts(line[1], "y", ny)
        low = in_order(line[0], low_x, "x", nx, 0)
        high = in_order(line[1], high_y, "y", ny, 0)
        low_y = shifts(low, "y", ny)
        high_x = shifts(high, "x", nx)
        low = in_order(low, low_y, "y", ny, 0)
        high = in_order(high, high_x, "x", nx, 1)
        return jnp.stack([low, high], 2).reshape(ny * nx * nc * line.shape[1], line.shape[2])

    def over_plane(full):
        line_rows = full.shape[0] // (ny * nx * nc)
        parts = full.reshape(ny, nx, nc, line_rows, full.shape[1])
        low = reduce_blocks(parts[:, :, 0], "x", nx, 1)
        high = reduce_blocks(parts[:, :, 1], "y", ny, 0)
        low, high = low.astype(BF16), high.astype(BF16)
        low = reduce_blocks(low, "y", ny, 0).astype(BF16)
        high = reduce_blocks(high, "x", nx, 0).astype(BF16)
        return jnp.stack([low, high], 0)

    def over_line(part):
        blocks = part.reshape(nc, ns, part.shape[1] // ns, part.shape[2])
        total = reduce_blocks(blocks, "seq", ns, 1)
        kept = pick(total, core_at, 0)
        came = swap(pick(total, nc - 1 - core_at, 0).astype(BF16)).astype(F32)
        low = jnp.where(core_at == 0, kept, came)
        high = jnp.where(core_at == 0, came, kept)
        return jnp.concatenate([low, high], 1)

    def to_owners(matrix, kept, count):
        came = [
            shift(matrix[d * count : (d + 1) * count], "seq", ns, d) for d in range(1, ns)
        ]
        return jnp.concatenate(ordered(kept, came[::-1], "seq", ns), 1)

    def to_heads(matrix):
        columns = matrix.shape[1] // ns

        def block(d):
            return lax.dynamic_slice_in_dim(
                matrix, lax.rem(seq_at + d, ns) * columns, columns, 1
            )

        sent = [block(d) for d in range(1, ns)]
        came = [shift(part, "seq", ns, d) for d, part in enumerate(sent, 1)]
        return jnp.concatenate([block(0)] + came[::-1], 0)

    by_owner = w_qkv.reshape(rows, 3, ns, own).transpose(0, 2, 1, 3).reshape(rows, 3 * width)
    to_owner = by_owner.reshape(rows, ns, 3 * own)
    kept = lax.dynamic_index_in_dim(to_owner, seq_at, 1, keepdims=False)
    came = [
        shift(
            lax.dynamic_index_in_dim(to_owner, lax.rem(seq_at + ns - d, ns), 1, keepdims=False),
            "seq", ns, ns - d,
        )
        for d in range(1, ns)
    ]
    own_line = in_order(kept, came, "seq", ns, 0).reshape(ns * rows, 3 * own)
    plane = gather_blocks(gather_blocks(own_line, "x", nx, 0), "y", ny, 0)
    own_qkv = gather_blocks(plane, "core", nc, 2).reshape(width, 3 * own)

    up_out = own_columns(w_up), own_columns(w_out)
    up_out = jnp.concatenate(up_out, 2)
    up_line = shifts(up_out, "seq", ns)
    small = (b_query, b_value, b_out, ln1_gain, ln1_shift, b_up, b_down, ln2_gain, ln2_shift)
    packed = jnp.concatenate((after(small[0], *up_line),) + small[1:])[None]
    packed = lax.all_to_all(
        jnp.tile(packed, (devices, 1)), ALL, split_axis=0, concat_axis=0, tiled=True
    ).astype(F32)
    vectors, place = [], 0
    for shard in small:
        vectors.append(packed[:, place : place + shard.shape[0]].reshape(-1))
        place += shard.shape[0]
    (bias_query, bias_value, bias_out, gain_one, shift_one, bias_up, bias_down, gain_two,
     shift_two) = vectors

    hidden_sent = after(hidden_states, *up_line)
    hidden_line = relayed(hidden_sent, "seq", ns)
    seq_hidden = jnp.concatenate([hidden_sent] + hidden_line, 0)
    down_own = after(own_columns(w_down), *hidden_line)
    down_line = shifts(down_own, "seq", ns)
    half_up_out = plane_of(line_of(up_out, up_line))
    half = inner_width // nc
    half_up, half_out = half_up_out[:, :half], half_up_out[:, half:]
    other_out = swap(half_out)
    half_down = plane_of(line_of(down_own, down_line))

    own_bias = jnp.concatenate(
        [
            lax.dynamic_slice_in_dim(bias_query, seq_at * own, own),
            jnp.zeros((own,), F32),
            lax.dynamic_slice_in_dim(bias_value, seq_at * own, own),
        ]
    )
    projected = (dot(seq_hidden, own_qkv) + own_bias).astype(BF16)
    outputs, log_total = attend_forward(projected)
    attn_tok = to_owners(outputs, outputs[:tokens], tokens)
    qkv_own = after(own_columns(by_owner), attn_tok)
    qkv_line = shifts(qkv_own, "seq", ns)
    half_qkv = plane_of(after(line_of(qkv_own, qkv_line), half_down))
    other_qkv = swap(half_qkv)

    mixed, mixed_other = dot(attn_tok, half_out), dot(attn_tok, other_out)
    mixed = jnp.concatenate(
        [
            jnp.where(core_at == 0, mixed, mixed_other),
            jnp.where(core_at == 0, mixed_other, mixed),
        ],
        1,
    )
    resid_one = hidden_states.astype(F32) + mixed + bias_out
    hidden_one, normed_one, inv_one = layer_norm(resid_one, gain_one, shift_one)
    hidden_low = hidden_one.astype(BF16)

    hidden_two = pair(hidden_low)
    inner = dot(hidden_two, half_up)
    gelu_value, gelu_slope = gelu_both(inner + halves(bias_up)[0])
    active_low = gelu_value.astype(BF16)
    resid_two = hidden_one + own_tokens(contract_last(active_low, half_down))
    layer_val, normed_two, inv_two = layer_norm(resid_two + bias_down, gain_two, shift_two)
    layer_out = layer_val.astype(BF16)

    grad_y = cotangent.astype(F32)
    grad_gain_two = jnp.sum(grad_y * normed_two, 0)
    grad_shift_two = jnp.sum(grad_y, 0)
    grad_resid_two = norm_back(grad_y, normed_two, inv_two, gain_two)
    grad_low_two = pair(grad_resid_two.astype(BF16))
    grad_bias_down = jnp.sum(grad_resid_two, 0)
    sum_down = contract_first(grad_low_two, active_low).astype(BF16)
    sum_down = over_plane(sum_down)
    grad_inner = dot(grad_low_two, half_down)
    grad_inner = grad_inner * gelu_slope
    grad_inner_low = grad_inner.astype(BF16)
    grad_bias_up = jnp.sum(grad_inner, 0)
    grad_hidden = grad_resid_two + own_tokens(contract_last(grad_inner_low, half_up))
    sum_up = contract_first(hidden_two, grad_inner_low).astype(BF16)
    sum_up = over_plane(sum_up)
    grad_gain_one = jnp.sum(grad_hidden * normed_one, 0)
    grad_shift_one = jnp.sum(grad_hidden, 0)
    grad_resid_one = norm_back(grad_hidden, normed_one, inv_one, gain_one)
    grad_low_one = grad_resid_one.astype(BF16)
    grad_bias_out = jnp.sum(grad_resid_one, 0)
    grad_kept, grad_sent = halves(grad_low_one)
    grad_attn = (
        contract_last(grad_kept, half_out) + contract_last(grad_sent, other_out)
    ).astype(BF16)
    grad_attn_cols = to_heads(grad_attn)
    grad_out_two = jnp.concatenate([grad_kept, swap(grad_sent)], 0)
    sum_out = contract_first(pair(attn_tok), grad_out_two).astype(BF16)
    sum_out = over_plane(sum_out)

    grad_own = attend_backward(projected, outputs, log_total, grad_attn_cols)
    grad_tok = to_owners(grad_own, grad_own[:tokens], tokens)
    own_kept, own_sent = halves(grad_own)
    other_sum = swap(contract_first(seq_hidden, own_sent).astype(BF16))
    sum_qkv = (contract_first(seq_hidden, own_kept) + other_sum.astype(F32)).astype(BF16)
    sum_qkv = over_plane(sum_qkv)
    to_core = pick(sum_qkv, nc - 1 - core_at, 0)
    sum_qkv = in_order(
        pick(sum_qkv, core_at, 0), [swap(to_core)], "core", nc, 1
    ).reshape(ns, rows, 3 * own)
    sum_qkv = in_order(
        pick(sum_qkv, seq_at, 0),
        [
            shift(pick(sum_qkv, lax.rem(seq_at + ns - d, ns), 0), "seq", ns, ns - d)
            for d in range(1, ns)
        ],
        "seq", ns, 0,
    )
    sum_qkv = sum_qkv.astype(F32).reshape(ns, rows, 3, own).transpose(1, 2, 0, 3)
    sum_qkv = sum_qkv.reshape(rows, 3 * width)
    tok_kept, tok_other = halves(grad_tok)
    grad_input = (
        grad_resid_one
        + contract_last(tok_kept, half_qkv)
        + contract_last(tok_other, other_qkv)
    )
    sum_down = over_line(after(sum_down, grad_attn_cols))
    sum_up = over_line(sum_up)
    sum_out = over_line(sum_out)

    def spread(part, whole, start):
        return lax.dynamic_update_slice_in_dim(jnp.zeros((whole,), F32), part, start, 0)

    own_sums = jnp.sum(grad_own.astype(F32), 0)

    def sum_small(parts):
        parts = lax.optimization_barrier(tuple(parts) + (grad_tok,))[:-1]
        stacked = jnp.concatenate([part.reshape(devices, -1) for part in parts], 1)
        arrived = lax.all_to_all(stacked, ALL, split_axis=0, concat_axis=0, tiled=True)
        total = jnp.sum(arrived, 0)
        ends, place = [], 0
        for part in parts:
            count = part.shape[0] // devices
            ends.append(total[place : place + count])
            place += count
        return ends

    (sum_gain_two, sum_shift_two, sum_bias_down, sum_bias_up, sum_gain_one, sum_shift_one,
     sum_bias_out, sum_bias_query, sum_bias_value) = sum_small(
        (grad_gain_two, grad_shift_two, grad_bias_down,
         spread(grad_bias_up, inner_width, core_at * half), grad_gain_one, grad_shift_one,
         grad_bias_out, spread(own_sums[:own], width, seq_at * own),
         spread(own_sums[2 * own :], width, seq_at * own))
    )
    return (layer_out, grad_input, sum_qkv, sum_bias_query, sum_bias_value, sum_out, sum_bias_out,
            sum_gain_one, sum_shift_one, sum_up, sum_bias_up, sum_down, sum_bias_down,
            sum_gain_two, sum_shift_two)


def solution(mesh):
    dp, ns = mesh.shape["dp"], mesh.shape["seq"]
    nc = 2
    ny = 2 if (dp // nc) % 2 == 0 else 1
    sizes = (ny, dp // (nc * ny), nc, ns)
    fine = Mesh(mesh.devices.reshape(sizes), ALL)
    matrix, vector = P(ALL, None), P(ALL)
    in_specs = (matrix, matrix, matrix, vector, vector, matrix, vector, vector, vector, matrix,
                vector, matrix, vector, vector, vector)
    out_specs = (matrix, matrix, matrix, vector, vector, matrix, vector, vector, vector, matrix,
                 vector, matrix, vector, vector, vector)

    def on_device(*args):
        return body(sizes, *args)

    return jax.shard_map(
        on_device, mesh=fine, in_specs=in_specs, out_specs=out_specs, check_vma=False
    )
```
